256 devices in a mesh: seq: 64 (over y, z, core), tensor: 4 (over x).
Axes of the slice: x: 4, y: 4, z: 8, core: 2. Of those that a mesh axis runs over, the one named last changes fastest.
Arguments:
- inputs: bfloat16 [2, 8192, 4096], P(None, 'seq', 'tensor'), may hold values from -600 to 600
- norm_gain: float32 [4096], replicated, may hold values from 0.1 to 1.9
- w_query: bfloat16 [4096, 2048], P('seq', 'tensor'), may hold values from -0.09375 to 0.09375
- w_key: bfloat16 [4096, 2048], P('seq', 'tensor'), may hold values from -0.09375 to 0.09375
- w_value: bfloat16 [4096, 2048], P('seq', 'tensor'), may hold values from -0.09375 to 0.09375
- random_head_directions: bfloat16 [16, 256, 128], P('tensor'), may hold values from -6 to 6
Outputs:
- attended: bfloat16 [2, 8192, 2048], P(None, 'seq', 'tensor')
The draws below stay inside these ranges and needn't reach their ends.
All inputs are finite; a program needn't handle non-finite values.
Results may differ from the reference program's by a relative error of at most 0.012.
The reference program's roundings to bfloat16 on the way count: a program that leaves them out, or rounds other values in their place, can miss the bound.
Values may be sent and summed in bfloat16 or wider, within the bound.
No kernel may reach another device: no remote copies, remote signals or barrier semaphores. Data moves between devices by JAX's collectives and lax.ppermute only.
A program may use at most 192 MiB of HBM per device.

```python
import math
import jax
import jax.numpy as jnp
from jax import lax

D = 4096
HEADS = 16
HEAD_SIZE = 128
M = 256
BATCH = 2
SEQ_DEV = 128
TOKEN_LENGTH = 8192
N_SEQ = 64


def draw_inputs(key, part):
    key_base, key_rows, key_cols = jax.random.split(key, 3)
    row_scale = jnp.exp(jax.random.uniform(key_rows, (BATCH, TOKEN_LENGTH, 1), jnp.float32) * math.log(10.0))
    col_scale = jnp.exp(jax.random.uniform(key_cols, (D,), jnp.float32) * math.log(10.0))
    base = jax.random.normal(key_base, (BATCH, TOKEN_LENGTH, D), jnp.float32)
    base = jnp.clip(base, -6.0, 6.0)
    return (base * row_scale * col_scale).astype(jnp.bfloat16)


def level_of(own_key, extent, shards, smallest, top_value):
    def one(axis_at, shards_of):
        heights = jax.random.uniform(jax.random.fold_in(jax.random.fold_in(own_key, 6), axis_at), (shards_of,), jnp.float32, smallest / len(shards), top_value / len(shards))
        return jnp.repeat(jnp.exp(heights), extent[axis_at] // shards_of).reshape((-1,) + (1,) * (len(extent) - axis_at - 1))

    level = one(*shards[0])
    for cut in shards[1:]:
        level = level * one(*cut)
    return level


def bell_draw(stream_key, shape, deviation, limit, cuts=(), kind=jnp.bfloat16):
    array = deviation * jax.random.normal(stream_key, shape, jnp.float32)
    if cuts:
        array = array * level_of(stream_key, shape, cuts, -0.22, 0.18)
    return jnp.clip(array, -limit, limit).astype(kind)


def setup_inputs(seed: int = 0) -> dict:
    splits = jax.random.split(jax.random.key(seed), 7)
    inputs = draw_inputs(jax.random.fold_in(splits[6], 71), 0)
    norm_gain = jnp.clip(1.0 + 0.18 * jax.random.normal(splits[1], (D,), jnp.float32), 0.1, 1.9)
    w_query = bell_draw(splits[2], (D, HEADS * HEAD_SIZE), D ** -0.5, 0.09375, ((0, 64), (1, 4)))
    w_key = bell_draw(splits[3], (D, HEADS * HEAD_SIZE), D ** -0.5, 0.09375, ((0, 64), (1, 4)))
    w_value = bell_draw(splits[4], (D, HEADS * HEAD_SIZE), D ** -0.5, 0.09375, ((0, 64), (1, 4)))
    random_head_directions = bell_draw(splits[5], (HEADS, M, HEAD_SIZE), 1.0, 6.0, ((0, 4),))
    return dict(inputs=inputs, norm_gain=norm_gain, w_query=w_query, w_key=w_key, w_value=w_value, random_head_directions=random_head_directions)


def rounded(values):
    return lax.optimization_barrier(values.astype(jnp.bfloat16)).astype(jnp.float32)

def feature_map(direction_product, random_head_directions):
    attention_logits = jnp.einsum('swcv,clv->swcl', direction_product, random_head_directions.astype(jnp.float32), precision=lax.Precision.HIGHEST) * HEAD_SIZE ** (-0.25)
    half_sq = 0.5 * lax.optimization_barrier(jnp.sum(direction_product * direction_product, axis=-1, keepdims=True)) * HEAD_SIZE ** (-0.5)
    return rounded(jnp.exp(attention_logits - half_sq) * M ** (-0.5))

def reference(inputs, norm_gain, w_query, w_key, w_value, random_head_directions):
    wide_in = inputs.astype(jnp.float32)
    inv_rms = lax.rsqrt(lax.optimization_barrier(jnp.mean(wide_in * wide_in, axis=-1, keepdims=True)) + 1e-05)
    normed = (wide_in * inv_rms * norm_gain).astype(jnp.bfloat16).reshape(BATCH * TOKEN_LENGTH, D)

    def project(weight):
        result = rounded(jnp.dot(normed, weight, preferred_element_type=jnp.float32))
        return jnp.moveaxis(result.reshape(BATCH, N_SEQ, SEQ_DEV, HEADS, HEAD_SIZE), 1, 0)
    query = project(w_query)
    keys = project(w_key)
    values = project(w_value)
    lower_triangle_mask = jnp.tril(jnp.ones((SEQ_DEV, SEQ_DEV), jnp.bool_))
    highest = lax.Precision.HIGHEST

    def block_step(carried, blocks):
        kv_state, key_sum = carried
        query_blk, key_blk, value_blk = blocks
        phi_query = feature_map(query_blk, random_head_directions)
        phi_key = feature_map(key_blk, random_head_directions)
        scores = jnp.where(lower_triangle_mask, jnp.einsum('bihm,bjhm->bhij', phi_query, phi_key, precision=highest), jnp.float32(0.0))
        denom_local = lax.optimization_barrier(jnp.sum(scores, axis=-1))
        numer_local = jnp.einsum('bhij,bjhd->bihd', rounded(scores), value_blk, precision=highest)
        numer_carried = jnp.einsum('bihm,bhmd->bihd', phi_query, rounded(kv_state), precision=highest)
        denom_carried = jnp.einsum('bihm,bhm->bih', phi_query, key_sum, precision=highest)
        numer = numer_local + numer_carried
        denom = jnp.transpose(denom_local, (0, 2, 1)) + denom_carried
        output = (numer / denom[..., None]).astype(jnp.bfloat16)
        kv_state = kv_state + jnp.einsum('bjhm,bjhd->bhmd', phi_key, value_blk, precision=highest)
        key_sum = key_sum + lax.optimization_barrier(jnp.sum(phi_key, axis=1))
        return ((kv_state, key_sum), output)
    initial = (jnp.zeros((BATCH, HEADS, M, HEAD_SIZE), jnp.float32), jnp.zeros((BATCH, HEADS, M), jnp.float32))
    finals, outputs = lax.scan(block_step, initial, (query, keys, values))
    return jnp.moveaxis(outputs, 0, 1).reshape(BATCH, TOKEN_LENGTH, HEADS * HEAD_SIZE)
```

```python
import jax
import jax.numpy as jnp
from jax import lax
from jax.sharding import PartitionSpec as P

F32 = jnp.float32
BF16 = jnp.bfloat16


def swap_pairs(count):
    return [(i, i ^ 1) for i in range(count)]


def ring(count, step):
    return [(i, (i + step) % count) for i in range(count)]


def gather_features(x, axis):
    count = lax.axis_size(axis)
    mine = lax.axis_index(axis)
    half = x.shape[0] // 2
    before = lax.ppermute(x, axis, ring(count, 1))
    after = lax.ppermute(x, axis, ring(count, -1))
    far_top = lax.ppermute(before[:half], axis, ring(count, 1))
    far_bottom = lax.ppermute(after[half:], axis, ring(count, -1))
    out = jnp.zeros((count,) + x.shape, x.dtype)
    out = lax.dynamic_update_slice(out, x[None], (mine, 0, 0))
    out = lax.dynamic_update_slice(out, before[None], ((mine + count - 1) % count, 0, 0))
    out = lax.dynamic_update_slice(out, after[None], ((mine + 1) % count, 0, 0))
    far = jnp.concatenate([far_top, far_bottom], axis=0)
    return lax.dynamic_update_slice(out, far[None], ((mine + 2) % count, 0, 0))


def feature_map(u, directions):
    head_dim = u.shape[-1]
    logits = jnp.einsum("bhtd,hmd->bhtm", u, directions, preferred_element_type=F32) * head_dim ** (-0.25)
    wide = u.astype(F32)
    half_sq = 0.5 * jnp.sum(wide * wide, axis=-1, keepdims=True) * head_dim ** (-0.5)
    return (jnp.exp(logits - half_sq) * directions.shape[1] ** (-0.5)).astype(BF16)


def split_two(total):
    high = total.astype(BF16)
    return high, (total - high.astype(F32)).astype(BF16)


def on_device(inputs, norm_gain, w_query, w_key, w_value, directions):
    seq_count = lax.axis_size("seq")
    chips = seq_count // 2
    core = lax.axis_index("seq") % 2
    same_core = [[2 * i + c for i in range(chips)] for c in range(2)]
    swap = swap_pairs(seq_count)
    batch, rows, width = inputs.shape
    tokens = batch * rows
    heads, features, head_dim = directions.shape
    half_heads = heads // 2
    half_cols = half_heads * head_dim

    def columns(which):
        parts = [lax.dynamic_slice_in_dim(w, which * half_cols, half_cols, 1) for w in (w_query, w_key, w_value)]
        return jnp.concatenate(parts, axis=1)

    own_rows = columns(core)
    other_rows = lax.ppermute(columns(1 - core), "seq", swap)
    chunk = jnp.where(
        core == 0,
        jnp.concatenate([own_rows, other_rows], axis=0),
        jnp.concatenate([other_rows, own_rows], axis=0),
    )
    weights = lax.all_gather(chunk, "seq", axis=0, tiled=True, axis_index_groups=same_core)

    gathered = gather_features(inputs.reshape(tokens, width), "tensor")
    parts = gathered.shape[0]
    wide = gathered.astype(F32)
    full_width = parts * width
    inv_rms = lax.rsqrt(jnp.sum(wide * wide, axis=(0, 2)) / full_width + 1e-05)
    gain = norm_gain.reshape(parts, 1, width)
    normed = (wide * inv_rms[None, :, None] * gain).astype(BF16)
    other_normed = lax.ppermute(normed, "seq", swap)
    both = jnp.concatenate(
        [
            normed.reshape(parts, batch, 1, rows, width),
            other_normed.reshape(parts, batch, 1, rows, width),
        ],
        axis=2,
    ).reshape(parts, 2 * tokens, width)
    accum = sum(
        jnp.dot(both[k], weights[k * width : (k + 1) * width], preferred_element_type=F32)
        for k in range(parts)
    )
    span = 2 * rows
    qkv = accum.astype(BF16).reshape(batch, span, 3, half_heads, head_dim)
    query, key, value = (jnp.transpose(qkv[:, :, i], (0, 2, 1, 3)) for i in range(3))

    my_directions = lax.dynamic_slice_in_dim(directions, core * half_heads, half_heads, 0)
    phi_key = feature_map(key, my_directions)
    state = jnp.einsum("bhjm,bhjd->bhmd", phi_key, value, preferred_element_type=F32)
    key_total = jnp.sum(phi_key.astype(F32), axis=2)

    per = batch * half_heads * features // chips
    high, low = split_two(key_total.reshape(chips, 1, per))
    key_row = jnp.concatenate(
        [high, low, jnp.zeros((chips, 1, head_dim - 2 * per), BF16)], axis=2
    )
    key_rows = jnp.pad(key_row, ((0, 0), (0, 7), (0, 0)))
    message = jnp.concatenate(
        [state.astype(BF16).reshape(chips, per, head_dim), key_rows], axis=1
    )
    arrived = lax.all_to_all(message, "seq", 0, 0, tiled=True, axis_index_groups=same_core)
    earlier = jnp.tril(jnp.ones((chips, chips), BF16), -1)
    prefix = jnp.einsum("ij,jrd->ird", earlier, arrived, preferred_element_type=F32)
    key_prefix = prefix[:, per, :per] + prefix[:, per, per : 2 * per]
    high, low = split_two(key_prefix)
    back_key = jnp.concatenate([high, low, jnp.zeros((chips, head_dim - 2 * per), BF16)], axis=1)
    back_keys = jnp.pad(back_key[:, None], ((0, 0), (0, 7), (0, 0)))
    reply = jnp.concatenate([prefix[:, :per].astype(BF16), back_keys], axis=1)
    returned = lax.all_to_all(reply, "seq", 0, 0, tiled=True, axis_index_groups=same_core)
    kv_rounded = returned[:, :per].reshape(batch, half_heads, features, head_dim)
    key_prefix = (
        returned[:, per, :per].astype(F32) + returned[:, per, per : 2 * per].astype(F32)
    ).reshape(batch, half_heads, features)

    phi_query = feature_map(query, my_directions)
    place = lax.broadcasted_iota(jnp.int32, (span, 1), 0)
    place = place % rows + jnp.where(place < rows, core, 1 - core) * rows
    causal = place >= place.reshape(1, span)
    scores = jnp.einsum("bhim,bhjm->bhij", phi_query, phi_key, preferred_element_type=F32)
    scores = jnp.where(causal, scores, F32(0.0))
    denom = jnp.sum(scores, axis=-1) + jnp.einsum(
        "bhim,bhm->bhi", phi_query.astype(F32), key_prefix, precision=lax.Precision.HIGHEST
    )
    numer = jnp.einsum("bhij,bhjd->bhid", scores.astype(BF16), value, preferred_element_type=F32)
    numer = numer + jnp.einsum("bhim,bhmd->bhid", phi_query, kv_rounded, preferred_element_type=F32)
    out = (numer / denom[..., None]).astype(BF16)
    out = jnp.transpose(out, (0, 2, 1, 3)).reshape(batch, 2, rows, half_cols)
    got = lax.ppermute(out[:, 1], "seq", swap)
    return jnp.where(
        core == 0,
        jnp.concatenate([out[:, 0], got], axis=-1),
        jnp.concatenate([got, out[:, 0]], axis=-1),
    )


def solution(mesh):
    in_specs = (
        P(None, "seq", "tensor"),
        P(),
        P("seq", "tensor"),
        P("seq", "tensor"),
        P("seq", "tensor"),
        P("tensor", None, None),
    )
    return jax.shard_map(
        on_device, mesh=mesh, in_specs=in_specs, out_specs=P(None, "seq", "tensor"), check_vma=False
    )
```
